32 devices in a mesh: grp: 2 (over y), seq: 8 (over z, x), head: 2 (over core).
Axes of the slice: x: 2, y: 2, z: 4, core: 2. Of those that a mesh axis runs over, the one named last changes fastest.
Arguments:
- queries: bfloat16 [2048, 32, 128], P(('grp', 'seq'), 'head'), parts along dimension 0, may hold values from -6 to 6
- new_keys: bfloat16 [2048, 4, 128], P(('grp', 'seq'), 'head'), parts along dimension 0, may hold values from -6 to 6
- incoming_values: bfloat16 [2048, 4, 128], P(('grp', 'seq'), 'head'), parts along dimension 0, may hold values from -6 to 6
- cache_pool_keys: bfloat16 [32, 128, 4, 128], P(('grp', 'seq'), None, 'head'), parts along dimension 0, may hold values from -6 to 6
- cache_pool_values: bfloat16 [32, 128, 4, 128], P(('grp', 'seq'), None, 'head'), parts along dimension 0, may hold values from -6 to 6
- prefix_block_table: int32 [8], P('grp'), parts along dimension 0, may hold values from 0 to 15, as said below
Outputs:
- attended: bfloat16 [2048, 4096], P(('grp', 'seq'), 'head'), parts along dimension 0
The draws below stay inside these ranges and needn't reach their ends.
There are 2 independent parts, one for each index of `grp`. The reference program is written for one: setup_inputs(seed, part) draws one part's arguments, and reference() takes and returns one part's arrays. A program takes and returns all parts, laid end to end along the dimension named above; each array names one. Nothing has to cross between parts.
Inputs may be any that keep to these rules, and one draw needn't show every extreme that they name: `prefix_block_table`: 4 distinct pool block numbers; block number b is held at position b % 2 by index b // 2 of seq, and no two entries are held by the same index.
All inputs are finite; a program needn't handle non-finite values.
Results may differ from the reference program's by a relative error of at most 0.008.
Values may be sent and summed in bfloat16 or wider, within the bound.
No kernel may reach another device: no remote copies, remote signals or barrier semaphores. Data moves between devices by JAX's collectives and lax.ppermute only.
A program may use at most 128 MiB of HBM per device.

```python
import math
import jax
import jax.numpy as jnp
from jax import lax

QUERY_HEADS = 32
KEY_VALUE_HEADS = 4
HEAD_SIZE = 128
BLOCK_TOKENS = 128
SLOTS = 2
NEW_TOKENS = 1024
NB = 4
PREFIX_TOKENS = 512
POOL_BLOCKS = 16


def draw_queries(key, part):
    value_rows = jax.random.normal(jax.random.fold_in(key, 11), (NEW_TOKENS, QUERY_HEADS, HEAD_SIZE), jnp.float32)
    return jnp.clip(value_rows, -6.0, 6.0).astype(jnp.bfloat16)


def draw_new_keys(key, part):
    value_rows = jax.random.normal(jax.random.fold_in(key, 12), (NEW_TOKENS, KEY_VALUE_HEADS, HEAD_SIZE), jnp.float32)
    return jnp.clip(value_rows, -6.0, 6.0).astype(jnp.bfloat16)


def draw_prefix_block_table(key, part):
    holders = POOL_BLOCKS // SLOTS
    order = jax.random.permutation(jax.random.fold_in(key, 21), holders)
    chosen = order[:NB].astype(jnp.int32)
    has_last = jnp.any(chosen == holders - 1)
    chosen = chosen.at[0].set(jnp.where(has_last, chosen[0], holders - 1))
    has_first = jnp.any(chosen == 0)
    spot = jnp.where(chosen[0] == holders - 1, 1, 0)
    chosen = chosen.at[spot].set(jnp.where(has_first, chosen[spot], 0))
    position = jax.random.randint(jax.random.fold_in(key, 22), (NB,), 0, SLOTS, jnp.int32)
    position = jnp.where(chosen == holders - 1, SLOTS - 1, position)
    position = jnp.where(chosen == 0, 0, position)
    return (chosen * SLOTS + position).astype(jnp.int32)


def block_levels(rng, extent, split, least, high):
    level = 1.0
    for axis_at, shards_of in split:
        heights = jax.random.uniform(jax.random.fold_in(jax.random.fold_in(rng, 6), axis_at), (shards_of,), jnp.float32, least / len(split), high / len(split))
        level = level * jnp.repeat(jnp.exp(heights), extent[axis_at] // shards_of).reshape((-1,) + (1,) * (len(extent) - 1 - axis_at))
    return level


def noise(rng, shape, scale, reach, shards=(), held_as=jnp.bfloat16):
    values = jax.random.normal(rng, shape, jnp.float32) * scale
    if len(shards) > 0:
        values = block_levels(rng, shape, shards, -0.22, 0.18) * values
    return jnp.clip(values, min=-reach, max=reach).astype(held_as)


def setup_inputs(seed: int = 0, part: int = 0) -> dict:
    keys = jax.random.split(jax.random.key(seed), 7)
    part_keys = jax.random.split(jax.random.fold_in(keys[6], part), 7)
    queries = draw_queries(jax.random.fold_in(jax.random.fold_in(keys[6], part), 71), part)
    new_keys = draw_new_keys(jax.random.fold_in(jax.random.fold_in(keys[6], part), 71), part)
    incoming_values = noise(part_keys[2], (NEW_TOKENS, KEY_VALUE_HEADS, HEAD_SIZE), 1.0, 6.0, ((0, 8), (1, 2)))
    cache_pool_keys = noise(part_keys[3], (POOL_BLOCKS, BLOCK_TOKENS, KEY_VALUE_HEADS, HEAD_SIZE), 1.0, 6.0, ((0, 8), (2, 2)))
    cache_pool_values = noise(part_keys[4], (POOL_BLOCKS, BLOCK_TOKENS, KEY_VALUE_HEADS, HEAD_SIZE), 1.0, 6.0, ((0, 8), (2, 2)))
    prefix_block_table = draw_prefix_block_table(jax.random.fold_in(jax.random.fold_in(keys[6], part), 71), part)
    return {"queries": queries, "new_keys": new_keys, "incoming_values": incoming_values, "cache_pool_keys": cache_pool_keys, "cache_pool_values": cache_pool_values, "prefix_block_table": prefix_block_table}


def reference(queries, new_keys, incoming_values, cache_pool_keys, cache_pool_values, prefix_block_table):
    query_groups = QUERY_HEADS // KEY_VALUE_HEADS
    scale = 1.0 / math.sqrt(HEAD_SIZE)
    gathered_prefix_keys = jnp.take(cache_pool_keys, prefix_block_table, axis=0).reshape(PREFIX_TOKENS, KEY_VALUE_HEADS, HEAD_SIZE)
    gathered_prefix_values = jnp.take(cache_pool_values, prefix_block_table, axis=0).reshape(PREFIX_TOKENS, KEY_VALUE_HEADS, HEAD_SIZE)
    all_keys = jnp.concatenate([gathered_prefix_keys, new_keys], axis=0).astype(jnp.float32)
    all_values = jnp.concatenate([gathered_prefix_values, incoming_values], axis=0).astype(jnp.float32)
    key_places = jnp.arange(PREFIX_TOKENS + NEW_TOKENS, dtype=jnp.int32) - PREFIX_TOKENS
    query_height = math.gcd(NEW_TOKENS, 256)
    grouped_queries = queries.reshape(NEW_TOKENS // query_height, query_height, KEY_VALUE_HEADS, query_groups, HEAD_SIZE)
    starts = (jnp.arange(NEW_TOKENS // query_height, dtype=jnp.int32) * query_height).astype(jnp.int32)

    def one_block(item):
        query_rows, start = item
        scores = jnp.einsum('rkgd,skd->rkgs', query_rows.astype(jnp.float32), all_keys) * scale
        row_places = start + jnp.arange(query_height, dtype=jnp.int32)
        visible = (key_places[None, :] <= row_places[:, None])[:, None, None, :]
        masked = jnp.where(visible, scores, -jnp.inf)
        top = lax.optimization_barrier(jnp.max(masked, axis=-1, keepdims=True))
        weights = jnp.where(visible, jnp.exp(masked - top), 0.0)
        total = lax.optimization_barrier(jnp.sum(weights, axis=-1))
        rounded = lax.optimization_barrier(weights.astype(jnp.bfloat16)).astype(jnp.float32)
        mixed = jnp.einsum('rkgs,skd->rkgd', rounded, all_values)
        return (mixed / total[..., None]).reshape(query_height, QUERY_HEADS * HEAD_SIZE).astype(jnp.bfloat16)
    return lax.map(one_block, (grouped_queries, starts)).reshape(NEW_TOKENS, QUERY_HEADS * HEAD_SIZE)
```

```python
import functools
import math

import jax
import jax.numpy as jnp
from jax import lax
from jax.experimental import pallas as pl
from jax.experimental.pallas import tpu as pltpu
from jax.sharding import PartitionSpec as P


neg_large = -1e30
VMEM = pltpu.VMEM


def holds(table_ref, device, slots):
    chosen = jnp.int32(0)
    slot = jnp.int32(0)
    for entry in range(table_ref.shape[0]):
        number = table_ref[entry]
        here = (number // slots) == device
        chosen = jnp.where(here, 1, chosen)
        slot = jnp.where(here, number % slots, slot)
    return chosen, slot


def pack_kernel(slots, table_ref, nk_ref, nv_ref, pk_ref, pv_ref, out_ref, kbuf, vbuf, wide, sems):
    me = lax.axis_index("seq")
    heads = out_ref.shape[0] // 4
    tokens = out_ref.shape[1]
    _, slot = holds(table_ref, me, slots)
    first = pltpu.make_async_copy(pk_ref.at[slot], kbuf, sems.at[0])
    second = pltpu.make_async_copy(pv_ref.at[slot], vbuf, sems.at[1])
    first.start()
    second.start()

    def spread(part, ref):
        wide[...] = ref[...].astype(jnp.float32)
        for head in range(heads):
            rows = wide[pl.ds(head, tokens, stride=heads), :]
            out_ref[part * heads + head] = rows.astype(jnp.bfloat16)

    spread(0, nk_ref)
    spread(1, nv_ref)
    first.wait()
    spread(2, kbuf)
    second.wait()
    spread(3, vbuf)


def pack(table, new_keys, new_values, pool_keys, pool_values):
    tokens, heads, width = new_keys.shape
    slots = pool_keys.shape[0]
    rows = tokens * heads
    anywhere = pl.BlockSpec(memory_space=pl.ANY)
    inside = pl.BlockSpec(memory_space=VMEM)
    return pl.pallas_call(
        functools.partial(pack_kernel, slots),
        out_shape=jax.ShapeDtypeStruct((4 * heads, tokens, width), jnp.bfloat16),
        in_specs=[pl.BlockSpec(memory_space=pltpu.SMEM), inside, inside, anywhere, anywhere],
        out_specs=inside,
        scratch_shapes=[
            VMEM((rows, width), jnp.bfloat16),
            VMEM((rows, width), jnp.bfloat16),
            VMEM((rows, width), jnp.float32),
            pltpu.SemaphoreType.DMA((2,)),
        ],
        compiler_params=pltpu.CompilerParams(vmem_limit_bytes=8 << 20),
    )(
        table,
        new_keys.reshape(rows, width),
        new_values.reshape(rows, width),
        pool_keys.reshape(slots, rows, width),
        pool_values.reshape(slots, rows, width),
    )


def attend_kernel(slots, heads, ranks, start, final, table_ref, *rest):
    count = len(ranks)
    rest = list(rest)
    if start:
        q_ref = rest.pop(0)
    else:
        qs, old_top, old_total, old_acc = rest[:4]
        rest = rest[4:]
    pieces = rest[:count]
    rest = rest[count:]
    tokens, width = pieces[0].shape[1], pieces[0].shape[2]
    if final:
        out_ref = rest.pop(0)
    elif start:
        qs, new_top, new_total, new_acc = rest[:4]
        rest = rest[4:]
    else:
        new_top, new_total, new_acc = rest[:3]
        rest = rest[3:]
    if start and final:
        qs = rest.pop(0)
    if start:
        wide = rest.pop(0)
    if final:
        new_top, new_total, new_acc = rest[:3]
        rest = rest[3:]
    scores = rest.pop(0)
    me = lax.axis_index("seq")
    rows = qs.shape[1]
    group = rows // tokens
    factor = math.log2(math.e) / math.sqrt(width)
    if start:
        wide[...] = q_ref[...].astype(jnp.float32)
    uses = []
    for place, k in enumerate(ranks):
        source = me ^ k
        chosen, _ = holds(table_ref, source, slots)
        uses.append((place, 0, source <= me, k == 0))
        uses.append((place, 1, chosen == 1, False))
    for head in range(heads):
        if start:
            for g in range(group):
                picked = wide[pl.ds(head * group + g, tokens, stride=heads * group), :]
                qs[head, g * tokens : (g + 1) * tokens, :] = picked.astype(jnp.bfloat16)
            new_top[head] = jnp.full((rows, tokens), neg_large, jnp.float32)
        else:
            new_top[head] = old_top[head]
        for spot, (place, part, used, causal) in enumerate(uses):

            @pl.when(used)
            def _():
                s = lax.dot_general(
                    qs[head],
                    pieces[place][part * 2 * heads + head],
                    (((1,), (1,)), ((), ())),
                    preferred_element_type=jnp.float32,
                )
                if causal:
                    s = s.reshape(group, tokens, tokens)
                    at = lax.broadcasted_iota(jnp.int32, s.shape, 1)
                    key_at = lax.broadcasted_iota(jnp.int32, s.shape, 2)
                    s = jnp.where(key_at <= at, s, neg_large).reshape(rows, tokens)
                scores[spot] = s
                new_top[head] = jnp.maximum(new_top[head], s)

        peak = jnp.max(new_top[head], axis=-1, keepdims=True)
        new_top[head] = jnp.broadcast_to(peak, (rows, tokens))
        if start:
            new_total[head] = jnp.zeros((rows, tokens), jnp.float32)
            new_acc[head] = jnp.zeros((rows, width), jnp.float32)
        else:
            fade = jnp.exp2((old_top[head] - new_top[head]) * factor)
            new_total[head] = old_total[head] * fade
            new_acc[head] = old_acc[head] * fade[:, :width]
        for spot, (place, part, used, _) in enumerate(uses):

            @pl.when(used)
            def _():
                p = jnp.exp2((scores[spot] - new_top[head]) * factor)
                new_total[head] += p
                new_acc[head] += jnp.dot(
                    p.astype(jnp.bfloat16),
                    pieces[place][part * 2 * heads + heads + head],
                    preferred_element_type=jnp.float32,
                )

        if final:
            whole = new_acc[head] / jnp.sum(new_total[head], axis=-1, keepdims=True)
            for g in range(group):
                column = (head * group + g) * width
                out_ref[:, column : column + width] = whole[g * tokens : (g + 1) * tokens].astype(
                    jnp.bfloat16
                )


def attend(table, queries, state, pieces, ranks, slots, start, final):
    tokens, query_heads, width = queries.shape
    heads = pieces[0].shape[0] // 4
    rows = query_heads // heads * tokens
    inside = pl.BlockSpec(memory_space=VMEM)
    qs = ((heads, rows, width), jnp.bfloat16)
    carried = [
        ((heads, rows, tokens), jnp.float32),
        ((heads, rows, tokens), jnp.float32),
        ((heads, rows, width), jnp.float32),
    ]
    scratch = []
    if start and final:
        scratch.append(qs)
    if start:
        scratch.append(((tokens * query_heads, width), jnp.float32))
    if final:
        scratch += carried
        outs = [((tokens, query_heads * width), jnp.bfloat16)]
    else:
        outs = ([qs] if start else []) + carried
    scratch.append(((2 * len(ranks), rows, tokens), jnp.float32))
    inputs = [queries.reshape(tokens * query_heads, width)] if start else list(state)
    bytes_of = lambda parts: sum(math.prod(s) * jnp.dtype(d).itemsize for s, d in parts)
    moved = bytes_of([(x.shape, x.dtype) for x in inputs + list(pieces)] + outs)
    work = 4 * len(ranks) * heads * rows * 2 * tokens * width
    result = pl.pallas_call(
        functools.partial(attend_kernel, slots, heads, ranks, start, final),
        out_shape=[jax.ShapeDtypeStruct(s, d) for s, d in outs],
        in_specs=[pl.BlockSpec(memory_space=pltpu.SMEM)] + [inside] * (len(inputs) + len(pieces)),
        out_specs=[inside] * len(outs),
        scratch_shapes=[VMEM(s, d) for s, d in scratch],
        cost_estimate=pl.CostEstimate(
            flops=work, bytes_accessed=moved, transcendentals=work // (4 * width)
        ),
        compiler_params=pltpu.CompilerParams(vmem_limit_bytes=(8 << 20) + moved + bytes_of(scratch)),
    )(table, *inputs, *pieces)
    if final:
        return result[0]
    return result if start else [state[0]] + list(result)


def move(x, n, k):
    return lax.ppermute(x, "seq", [(i, i ^ k) for i in range(n)])


def body(n, queries, new_keys, new_values, pool_keys, pool_values, table):
    own = pack(table, new_keys, new_values, pool_keys, pool_values)
    pieces = {0: own}
    quad = min(n, 4)
    for k in range(quad, n, quad):
        pieces[k] = move(own, n, k)
    for low in (3, 2, 1):
        if low < quad:
            pieces[low] = move(own, n, low)
    for k in range(quad, n, quad):
        for low in (3, 2, 1):
            if low < quad:
                pieces[k + low] = move(pieces[k], n, low)
    groups = [(0,)] + [
        tuple(range(first, min(first + quad, n))) for first in range(1, n, quad)
    ]
    state = None
    for number, ranks in enumerate(groups):
        state = attend(
            table,
            queries,
            state,
            [pieces[k] for k in ranks],
            ranks,
            pool_keys.shape[0],
            number == 0,
            number == len(groups) - 1,
        )
    return state


def solution(mesh):
    in_specs = (
        P(("grp", "seq"), "head", None),
        P(("grp", "seq"), "head", None),
        P(("grp", "seq"), "head", None),
        P(("grp", "seq"), None, "head", None),
        P(("grp", "seq"), None, "head", None),
        P("grp"),
    )
    out_specs = P(("grp", "seq"), "head")
    return jax.shard_map(
        functools.partial(body, mesh.shape["seq"]),
        mesh=mesh,
        in_specs=in_specs,
        out_specs=out_specs,
        check_vma=False,
    )
```

```python
import functools
import math

import jax
import jax.numpy as jnp
from jax import lax
from jax.experimental import pallas as pl
from jax.experimental.pallas import tpu as pltpu
from jax.sharding import PartitionSpec as P


neg_large = -1e30
VMEM = pltpu.VMEM


def holds(table_ref, device, slots):
    chosen = jnp.int32(0)
    slot = jnp.int32(0)
    for entry in range(table_ref.shape[0]):
        number = table_ref[entry]
        here = (number // slots) == device
        chosen = jnp.where(here, 1, chosen)
        slot = jnp.where(here, number % slots, slot)
    return chosen, slot


def stay(x):
    return pltpu.with_memory_space_constraint(x, pltpu.HBM)


def pack_kernel(slots, table_ref, nk_ref, nv_ref, pk_ref, pv_ref, out_ref, raw, wide, sems):
    me = lax.axis_index("seq")
    heads = out_ref.shape[0] // 4
    tokens = out_ref.shape[1]
    _, slot = holds(table_ref, me, slots)
    sources = [nk_ref, nv_ref, pk_ref.at[slot], pv_ref.at[slot]]
    copies = [
        pltpu.make_async_copy(source, raw.at[part], sems.at[part])
        for part, source in enumerate(sources)
    ]
    for copy in copies:
        copy.start()
    for part, copy in enumerate(copies):
        copy.wait()
        wide[part] = raw[part].astype(jnp.float32)
        for head in range(heads):
            rows = wide[part, pl.ds(head, tokens, stride=heads), :]
            out_ref[part * heads + head] = rows.astype(jnp.bfloat16)


def pack(table, new_keys, new_values, pool_keys, pool_values):
    tokens, heads, width = new_keys.shape
    slots = pool_keys.shape[0]
    rows = tokens * heads
    far = pl.BlockSpec(memory_space=pltpu.HBM)
    return pl.pallas_call(
        functools.partial(pack_kernel, slots),
        out_shape=jax.ShapeDtypeStruct((4 * heads, tokens, width), jnp.bfloat16),
        in_specs=[pl.BlockSpec(memory_space=pltpu.SMEM), far, far, far, far],
        out_specs=pl.BlockSpec(memory_space=VMEM),
        scratch_shapes=[
            VMEM((4, rows, width), jnp.bfloat16),
            VMEM((4, rows, width), jnp.float32),
            pltpu.SemaphoreType.DMA((4,)),
        ],
        compiler_params=pltpu.CompilerParams(vmem_limit_bytes=8 << 20),
    )(
        table,
        stay(new_keys.reshape(rows, width)),
        stay(new_values.reshape(rows, width)),
        stay(pool_keys.reshape(slots, rows, width)),
        stay(pool_values.reshape(slots, rows, width)),
    )


def attend_kernel(slots, heads, ranks, start, final, table_ref, *rest):
    count = len(ranks)
    rest = list(rest)
    if start:
        q_ref = rest.pop(0)
    else:
        qs, old_top, old_total, old_acc = rest[:4]
        rest = rest[4:]
    pieces = rest[:count]
    rest = rest[count:]
    tokens, width = pieces[0].shape[1], pieces[0].shape[2]
    if final:
        out_ref = rest.pop(0)
    elif start:
        qs, new_top, new_total, new_acc = rest[:4]
        rest = rest[4:]
    else:
        new_top, new_total, new_acc = rest[:3]
        rest = rest[3:]
    if start and final:
        qs = rest.pop(0)
    if start:
        wide = rest.pop(0)
    if final:
        new_top, new_total = rest[:2]
        rest = rest[2:]
    scores, rounded = rest
    me = lax.axis_index("seq")
    rows = qs.shape[1]
    group = rows // tokens
    factor = math.log2(math.e) / math.sqrt(width)
    if start:
        wide[...] = q_ref[...].astype(jnp.float32)
    uses = []
    for place, k in enumerate(ranks):
        source = me ^ k
        chosen, _ = holds(table_ref, source, slots)
        bias = jnp.where(source <= me, 0.0, neg_large).astype(jnp.float32)
        uses.append((place, 0, bias, k == 0))
        bias = jnp.where(chosen == 1, 0.0, neg_large).astype(jnp.float32)
        uses.append((place, 1, bias, False))
    keys_of = lambda head, use: pieces[use[0]][use[1] * 2 * heads + head]
    values_of = lambda head, use: pieces[use[0]][use[1] * 2 * heads + heads + head]
    tall = min(rows, 256)
    small = 64
    for head in range(heads):
        if start:
            for g in range(group):
                picked = wide[pl.ds(head * group + g, tokens, stride=heads * group), :]
                qs[head, g * tokens : (g + 1) * tokens, :] = picked.astype(jnp.bfloat16)
        for pair in range(0, len(uses), 2):
            keys = jnp.concatenate([keys_of(head, use) for use in uses[pair : pair + 2]], axis=0)
            for low in range(0, rows, tall):
                s = lax.dot_general(
                    qs[head, low : low + tall, :],
                    keys,
                    (((1,), (1,)), ((), ())),
                    preferred_element_type=jnp.float32,
                )
                for half, use in enumerate(uses[pair : pair + 2]):
                    part = s[:, half * tokens : (half + 1) * tokens] * factor
                    if use[3]:
                        part = part.reshape(tall // tokens, tokens, tokens)
                        at = lax.broadcasted_iota(jnp.int32, part.shape, 1)
                        key_at = lax.broadcasted_iota(jnp.int32, part.shape, 2)
                        part = jnp.where(key_at <= at, part, neg_large).reshape(tall, tokens)
                    else:
                        part = part + use[2]
                    column = (pair + half) * tokens
                    scores[low : low + tall, column : column + tokens] = part
        for low in range(0, rows, small):
            span = slice(low, low + small)
            tiles = [
                scores[span, spot * tokens : (spot + 1) * tokens] for spot in range(len(uses))
            ]
            peak = functools.reduce(jnp.maximum, tiles)
            if not start:
                peak = jnp.maximum(peak, old_top[head, span, :])
            peak = jnp.max(peak, axis=-1, keepdims=True)
            peak = jnp.broadcast_to(peak, (small, tokens))
            weights = [jnp.exp2(tile - peak) for tile in tiles]
            sums = functools.reduce(jnp.add, weights)
            if not start:
                fade = jnp.exp2(old_top[head, span, :] - peak)
                sums = sums + old_total[head, span, :] * fade
            new_top[head, span, :] = peak
            new_total[head, span, :] = sums
            for spot, p in enumerate(weights):
                rounded[span, spot * tokens : (spot + 1) * tokens] = p.astype(jnp.bfloat16)
        values = jnp.concatenate([values_of(head, use) for use in uses], axis=0)
        for low in range(0, rows, tall):
            span = slice(low, low + tall)
            mixed = jnp.dot(rounded[span, :], values, preferred_element_type=jnp.float32)
            if not start:
                fade = jnp.exp2(old_top[head, span, :] - new_top[head, span, :])
                mixed = mixed + old_acc[head, span, :] * fade[:, :width]
            if not final:
                new_acc[head, span, :] = mixed
                continue
            whole = mixed / jnp.sum(new_total[head, span, :], axis=-1, keepdims=True)
            for g in range(low // tokens, (low + tall) // tokens):
                column = (head * group + g) * width
                inner = slice(g * tokens - low, (g + 1) * tokens - low)
                out_ref[:, column : column + width] = whole[inner].astype(jnp.bfloat16)


def attend(table, queries, state, pieces, ranks, slots, start, final):
    tokens, query_heads, width = queries.shape
    heads = pieces[0].shape[0] // 4
    rows = query_heads // heads * tokens
    inside = pl.BlockSpec(memory_space=VMEM)
    qs = ((heads, rows, width), jnp.bfloat16)
    carried = [
        ((heads, rows, tokens), jnp.float32),
        ((heads, rows, tokens), jnp.float32),
        ((heads, rows, width), jnp.float32),
    ]
    scratch = []
    if start and final:
        scratch.append(qs)
    if start:
        scratch.append(((tokens * query_heads, width), jnp.float32))
    if final:
        scratch += carried[:2]
        outs = [((tokens, query_heads * width), jnp.bfloat16)]
    else:
        outs = ([qs] if start else []) + carried
    scratch.append(((rows, 2 * len(ranks) * tokens), jnp.float32))
    scratch.append(((rows, 2 * len(ranks) * tokens), jnp.bfloat16))
    inputs = [queries.reshape(tokens * query_heads, width)] if start else list(state)
    bytes_of = lambda parts: sum(math.prod(s) * jnp.dtype(d).itemsize for s, d in parts)
    moved = bytes_of([(x.shape, x.dtype) for x in inputs + list(pieces)] + outs)
    work = 4 * len(ranks) * heads * rows * 2 * tokens * width
    result = pl.pallas_call(
        functools.partial(attend_kernel, slots, heads, ranks, start, final),
        out_shape=[jax.ShapeDtypeStruct(s, d) for s, d in outs],
        in_specs=[pl.BlockSpec(memory_space=pltpu.SMEM)] + [inside] * (len(inputs) + len(pieces)),
        out_specs=[inside] * len(outs),
        scratch_shapes=[VMEM(s, d) for s, d in scratch],
        cost_estimate=pl.CostEstimate(
            flops=work, bytes_accessed=moved, transcendentals=work // (4 * width)
        ),
        compiler_params=pltpu.CompilerParams(vmem_limit_bytes=(8 << 20) + moved + bytes_of(scratch)),
    )(table, *inputs, *pieces)
    if final:
        return result[0]
    return result if start else [state[0]] + list(result)


def move(x, n, k):
    return lax.ppermute(x, "seq", [(i, i ^ k) for i in range(n)])


def body(n, queries, new_keys, new_values, pool_keys, pool_values, table):
    table = stay(table)
    own = pack(table, new_keys, new_values, pool_keys, pool_values)
    pieces = {0: own}
    quad = min(n, 4)
    for k in range(quad, n, quad):
        pieces[k] = move(own, n, k)
    for low in (3, 2, 1):
        if low < quad:
            pieces[low] = move(own, n, low)
    for k in range(quad, n, quad):
        for low in (3, 2, 1):
            if low < quad:
                pieces[k + low] = move(pieces[k], n, low)
    groups = [(0,)] + [
        tuple(range(first, min(first + quad, n))) for first in range(1, n, quad)
    ]
    state = None
    for number, ranks in enumerate(groups):
        state = attend(
            table,
            queries,
            state,
            [pieces[k] for k in ranks],
            ranks,
            pool_keys.shape[0],
            number == 0,
            number == len(groups) - 1,
        )
    return state


def solution(mesh):
    in_specs = (
        P(("grp", "seq"), "head", None),
        P(("grp", "seq"), "head", None),
        P(("grp", "seq"), "head", None),
        P(("grp", "seq"), None, "head", None),
        P(("grp", "seq"), None, "head", None),
        P("grp"),
    )
    out_specs = P(("grp", "seq"), "head")
    return jax.shard_map(
        functools.partial(body, mesh.shape["seq"]),
        mesh=mesh,
        in_specs=in_specs,
        out_specs=out_specs,
        check_vma=False,
    )
```

```python
import functools
import math

import jax
import jax.numpy as jnp
from jax import lax
from jax.experimental import pallas as pl
from jax.experimental.pallas import tpu as pltpu
from jax.sharding import PartitionSpec as P


neg_large = -1e30
VMEM = pltpu.VMEM


def holds(table_ref, device, slots):
    chosen = jnp.int32(0)
    slot = jnp.int32(0)
    for entry in range(table_ref.shape[0]):
        number = table_ref[entry]
        here = (number // slots) == device
        chosen = jnp.where(here, 1, chosen)
        slot = jnp.where(here, number % slots, slot)
    return chosen, slot


def stay(x):
    return pltpu.with_memory_space_constraint(x, pltpu.HBM)


def pack_kernel(
    slots, table_ref, nk_ref, nv_ref, pk_ref, pv_ref, out_ref, fresh_ref, block_ref, raw, wide, sems
):
    me = lax.axis_index("seq")
    heads = out_ref.shape[0] // 4
    tokens = out_ref.shape[1]
    _, slot = holds(table_ref, me, slots)
    sources = [nk_ref, nv_ref, pk_ref.at[slot], pv_ref.at[slot]]
    copies = [
        pltpu.make_async_copy(source, raw.at[part], sems.at[part])
        for part, source in enumerate(sources)
    ]
    for copy in copies:
        copy.start()
    for part, copy in enumerate(copies):
        copy.wait()
        wide[part] = raw[part].astype(jnp.float32)
        for head in range(heads):
            rows = wide[part, pl.ds(head, tokens, stride=heads), :]
            if part % 2:
                rows = rows.T
            rows = rows.astype(jnp.bfloat16)
            out_ref[part * heads + head] = rows
            single = block_ref if part >= 2 else fresh_ref
            single[part % 2 * heads + head] = rows


def pack(table, new_keys, new_values, pool_keys, pool_values):
    tokens, heads, width = new_keys.shape
    slots = pool_keys.shape[0]
    rows = tokens * heads
    far = pl.BlockSpec(memory_space=pltpu.HBM)
    return pl.pallas_call(
        functools.partial(pack_kernel, slots),
        out_shape=[
            jax.ShapeDtypeStruct((parts * heads, tokens, width), jnp.bfloat16)
            for parts in (4, 2, 2)
        ],
        in_specs=[pl.BlockSpec(memory_space=pltpu.SMEM), far, far, far, far],
        out_specs=[pl.BlockSpec(memory_space=VMEM)] * 3,
        scratch_shapes=[
            VMEM((4, rows, width), jnp.bfloat16),
            VMEM((4, rows, width), jnp.float32),
            pltpu.SemaphoreType.DMA((4,)),
        ],
        compiler_params=pltpu.CompilerParams(vmem_limit_bytes=8 << 20),
    )(
        table,
        stay(new_keys.reshape(rows, width)),
        stay(new_values.reshape(rows, width)),
        stay(pool_keys.reshape(slots, rows, width)),
        stay(pool_values.reshape(slots, rows, width)),
    )


def attend_kernel(slots, heads, uses, blocks, count, start, final, table_ref, *rest):
    rest = list(rest)
    if start:
        q_ref = rest.pop(0)
    else:
        qs, old_top, old_total, old_acc = rest[:4]
        rest = rest[4:]
    pieces = rest[:count]
    rest = rest[count:]
    if final:
        out_ref = rest.pop(0)
    elif start:
        qs, new_top, new_total, new_acc = rest[:4]
        rest = rest[4:]
    else:
        new_top, new_total, new_acc = rest[:3]
        rest = rest[3:]
    if start and final:
        qs = rest.pop(0)
    if start:
        wide = rest.pop(0)
    if final:
        ready, sems = rest[:2]
        rest = rest[2:]
    scores, rounded, chosen = rest
    me = lax.axis_index("seq")
    _, tokens, width = pieces[0].shape
    rows = qs.shape[1]
    group = rows // tokens
    factor = math.log2(math.e) / math.sqrt(width)
    if start:
        wide[...] = q_ref[...].astype(jnp.float32)
        for at in range(heads * group):
            picked = wide[pl.ds(at, tokens, stride=heads * group), :].astype(jnp.bfloat16)
            qs[at // group, at % group * tokens : (at % group + 1) * tokens, :] = picked
    slot = jnp.int32(0)
    for place, base, k in blocks:
        used, _ = holds(table_ref, me ^ k, slots)

        @pl.when(used == 1)
        def _():
            chosen[slot] = pieces[place][base : base + 2 * heads]

        slot = jnp.minimum(slot + used, chosen.shape[0] - 1)
    tiles = [(pieces[place], base, k) for place, base, k in uses]
    if blocks:
        tiles += [(chosen.at[at], 0, None) for at in range(chosen.shape[0])]
    allowed = [None if k is None or k == 0 else (me ^ k) <= me for _, _, k in tiles]
    span = min(rows, 2 * tokens)
    folded = lambda x: x.reshape(tokens // 8, 8, span)
    turns = [(head, low) for head in range(heads) for low in range(0, rows, span)]
    peaks, totals, copies = {}, {}, []

    def score(turn):
        head, low = turns[turn]
        here = slice(low, low + span)
        queries = qs[head, here, :]
        peak = None
        for pair in range(0, len(tiles), 2):
            both = tiles[pair : pair + 2]
            keys = jnp.concatenate([ref[base + head] for ref, base, _ in both], axis=0)
            s = lax.dot_general(
                keys, queries, (((1,), (1,)), ((), ())), preferred_element_type=jnp.float32
            )
            for half, (_, _, k) in enumerate(both):
                part = s[half * tokens : (half + 1) * tokens] * factor
                if k == 0:
                    key_at = lax.broadcasted_iota(jnp.int32, part.shape, 0)
                    at = lax.broadcasted_iota(jnp.int32, part.shape, 1) % tokens
                    part = jnp.where(key_at <= at, part, neg_large)
                scores[turn % 2, pair + half] = part
                most = jnp.max(folded(part), axis=0)
                if allowed[pair + half] is not None:
                    most = jnp.where(allowed[pair + half], most, neg_large)
                peak = most if peak is None else jnp.maximum(peak, most)
        peak = jnp.max(peak, axis=0, keepdims=True)
        if not start:
            peak = jnp.maximum(peak, old_top[head, :, here])
        peaks[turn] = peak

    def weigh(turn):
        peak = peaks[turn]
        sums = jnp.zeros((8, span), jnp.float32)
        for at in range(len(tiles)):
            level = peak
            if allowed[at] is not None:
                level = jnp.where(allowed[at], peak, -neg_large)
            p = jnp.exp2(scores[turn % 2, at] - level)
            sums = sums + jnp.sum(folded(p), axis=0)
            rounded[turn % 2, at * tokens : (at + 1) * tokens, :] = p.astype(jnp.bfloat16)
        totals[turn] = jnp.sum(sums, axis=0, keepdims=True)

    def mix(turn):
        head, low = turns[turn]
        here = slice(low, low + span)
        peak, sums = peaks[turn], totals[turn]
        values = jnp.concatenate([ref[base + heads + head] for ref, base, _ in tiles], axis=1)
        mixed = jnp.dot(values, rounded[turn % 2], preferred_element_type=jnp.float32)
        if not start:
            fade = jnp.exp2(old_top[head, :, here] - peak)
            sums = sums + old_total[head, :, here] * fade
            mixed = mixed + old_acc[head, :, here] * fade
        if not final:
            new_top[head, :, here] = peak
            new_total[head, :, here] = sums
            new_acc[head, :, here] = mixed
            return
        whole = (mixed * (1.0 / sums)).astype(jnp.bfloat16)
        for inner in range(0, span, tokens):
            column = (head * group + (low + inner) // tokens) * width
            ready[:, column : column + width] = whole[:, inner : inner + tokens].T
        if low + span == rows:
            columns = pl.ds(head * group * width, group * width)
            copies.append(
                pltpu.make_async_copy(ready.at[:, columns], out_ref.at[:, columns], sems.at[head])
            )
            copies[-1].start()

    for turn in range(len(turns) + 2):
        if turn < len(turns):
            score(turn)
        if 0 <= turn - 1 < len(turns):
            weigh(turn - 1)
        if turn >= 2:
            mix(turn - 2)
    for copy in copies:
        copy.wait()


def attend(table, queries, state, chunks, heads, slots, start, final):
    tokens, query_heads, width = queries.shape
    rows = query_heads // heads * tokens
    span = min(rows, 2 * tokens)
    pieces, uses, blocks = [], [], []
    for array, base, k, block in chunks:
        places = [at for at, held in enumerate(pieces) if held is array]
        if not places:
            places = [len(pieces)]
            pieces.append(array)
        (blocks if block else uses).append((places[0], base, k))
    taken = table.shape[0]
    inside = pl.BlockSpec(memory_space=VMEM)
    qs = ((heads, rows, width), jnp.bfloat16)
    carried = [
        ((heads, 1, rows), jnp.float32),
        ((heads, 1, rows), jnp.float32),
        ((heads, width, rows), jnp.float32),
    ]
    out = ((tokens, query_heads * width), jnp.bfloat16)
    tiles = len(uses) + (taken if blocks else 0)
    scratch = []
    if start and final:
        scratch.append(qs)
    if start:
        scratch.append(((tokens * query_heads, width), jnp.float32))
    if final:
        scratch.append(out)
    tail = [
        ((2, tiles, tokens, span), jnp.float32),
        ((2, tiles * tokens, span), jnp.bfloat16),
        ((taken if blocks else 1, 2 * heads, tokens, width), jnp.bfloat16),
    ]
    inputs = [queries.reshape(tokens * query_heads, width)] if start else list(state)
    outs = [out] if final else ([qs] if start else []) + carried
    bytes_of = lambda parts: sum(math.prod(s) * jnp.dtype(d).itemsize for s, d in parts)
    moved = bytes_of([(x.shape, x.dtype) for x in inputs + pieces] + outs)
    work = 2 * tiles * heads * rows * 2 * tokens * width
    result = pl.pallas_call(
        functools.partial(attend_kernel, slots, heads, uses, blocks, len(pieces), start, final),
        out_shape=[jax.ShapeDtypeStruct(s, d) for s, d in outs],
        in_specs=[pl.BlockSpec(memory_space=pltpu.SMEM)] + [inside] * (len(inputs) + len(pieces)),
        out_specs=[pl.BlockSpec(memory_space=pltpu.HBM)] if final else [inside] * len(outs),
        scratch_shapes=[VMEM(s, d) for s, d in scratch]
        + ([pltpu.SemaphoreType.DMA((heads,))] if final else [])
        + [VMEM(s, d) for s, d in tail],
        cost_estimate=pl.CostEstimate(
            flops=work, bytes_accessed=moved, transcendentals=work // (4 * width)
        ),
        compiler_params=pltpu.CompilerParams(
            vmem_limit_bytes=(8 << 20) + moved + bytes_of(scratch + tail)
        ),
    )(table, *inputs, *pieces)
    if final:
        return result[0]
    return result if start else [state[0]] + list(result)


def move(x, n, k, sends=lambda i: True):
    return lax.ppermute(x, "seq", [(i, i ^ k) for i in range(n) if sends(i)])


def plan(n):
    far = range(4, n, 4)
    lows = (3, 1, 2)
    most = 6
    split = lambda items: [items[at : at + most] for at in range(0, len(items), most)]
    groups = [[(0, False)]]
    groups += split([(1, False), (2, False)])
    groups += [[(k, True) for k in range(n)] + [(k, False) for k in far[:1]] + [(3, False)]]
    groups += split([(k, False) for k in far[1:]])
    groups += split([(k + low, False) for k in far for low in lows])
    return far, lows, groups


def body(n, queries, new_keys, new_values, pool_keys, pool_values, table):
    heads = new_keys.shape[1]
    slots = pool_keys.shape[0]
    table = stay(table)
    far, lows, groups = plan(n)
    own, fresh, block = pack(table, new_keys, new_values, pool_keys, pool_values)
    held = {(0, False): (own, 0), (0, True): (own, 2 * heads)}

    def keep(k, array):
        held[(k, False)] = (array, 0)
        held[(k, True)] = (array, 2 * heads)

    for k in far:
        held[(k, True)] = (move(block, n, k), 0)
    beside = move(own, n, 1)
    below = move(own, n, 2)
    keep(1, beside)
    keep(2, below)
    for k in far:
        held[(k, False)] = (move(fresh, n, k, lambda i: i ^ k > i), 0)
    for k in far:
        for low in lows:
            got = move(held[(k, True)][0], n, low)
            held[(k + low, True)] = (got, 0)
    keep(3, move(below, n, 1))
    for k in far:
        for low in lows:
            got = move(held[(k, False)][0], n, low, lambda i: i ^ k < i)
            held[(k + low, False)] = (got, 0)
    state = None
    for number, group in enumerate(groups):
        state = attend(
            table,
            queries,
            state,
            [held[chunk] + chunk for chunk in group],
            heads,
            slots,
            number == 0,
            number == len(groups) - 1,
        )
    return state


def solution(mesh):
    in_specs = (
        P(("grp", "seq"), "head", None),
        P(("grp", "seq"), "head", None),
        P(("grp", "seq"), "head", None),
        P(("grp", "seq"), None, "head", None),
        P(("grp", "seq"), None, "head", None),
        P("grp"),
    )
    out_specs = P(("grp", "seq"), "head")
    n = mesh.shape["seq"]
    return jax.shard_map(
        functools.partial(body, n),
        mesh=mesh,
        in_specs=in_specs,
        out_specs=out_specs,
        check_vma=False,
    )
```

```python
import functools
import math

import jax
import jax.numpy as jnp
from jax import lax
from jax.experimental import pallas as pl
from jax.experimental.pallas import tpu as pltpu
from jax.sharding import PartitionSpec as P


neg_large = -1e30
VMEM = pltpu.VMEM


def holds(table_ref, device, slots):
    chosen = jnp.int32(0)
    slot = jnp.int32(0)
    for entry in range(table_ref.shape[0]):
        number = table_ref[entry]
        here = (number // slots) == device
        chosen = jnp.where(here, 1, chosen)
        slot = jnp.where(here, number % slots, slot)
    return chosen, slot


def stay(x):
    return pltpu.with_memory_space_constraint(x, pltpu.HBM)


def pack_kernel(
    peers, table_ref, nk_ref, nv_ref, pk_ref, pv_ref, out_ref, fresh_ref, block_ref, *rest
):
    flags_ref, *scratch = rest
    numbers, fresh, pool, wide, sems = scratch
    me = lax.axis_index("seq")
    heads = out_ref.shape[0] // 4
    tokens = out_ref.shape[1]
    copies = [
        pltpu.make_async_copy(source, target, sems.at[at])
        for at, (source, target) in enumerate(
            [
                (table_ref, numbers),
                (pk_ref, pool.at[0]),
                (pv_ref, pool.at[1]),
                (nk_ref, fresh.at[0]),
                (nv_ref, fresh.at[1]),
            ]
        )
    ]
    for copy in copies:
        copy.start()
    copies[0].wait()
    _, slot = holds(numbers, me, pool.shape[1])
    for part in (2, 3, 0, 1):
        if part >= 2:
            copies[part - 1].wait()
            wide[part] = pool[part - 2, slot].astype(jnp.float32)
        else:
            copies[part + 3].wait()
            wide[part] = fresh[part].astype(jnp.float32)
        for head in range(heads):
            rows = wide[part, pl.ds(head, tokens, stride=heads), :]
            if part % 2:
                rows = rows.T
            rows = rows.astype(jnp.bfloat16)
            out_ref[part * heads + head] = rows
            single = block_ref if part >= 2 else fresh_ref
            single[part % 2 * heads + head] = rows
    at = lax.broadcasted_iota(jnp.int32, flags_ref.shape, 1)
    flags = jnp.zeros(flags_ref.shape, jnp.int32)
    for k in range(peers):
        flags = jnp.where(at == k, holds(numbers, me ^ k, pool.shape[1])[0], flags)
    flags_ref[...] = flags


def pack(peers, table, new_keys, new_values, pool_keys, pool_values):
    tokens, heads, width = new_keys.shape
    slots = pool_keys.shape[0]
    rows = tokens * heads
    far = pl.BlockSpec(memory_space=pltpu.HBM)
    return pl.pallas_call(
        functools.partial(pack_kernel, peers),
        out_shape=[
            jax.ShapeDtypeStruct((parts * heads, tokens, width), jnp.bfloat16)
            for parts in (4, 2, 2)
        ]
        + [jax.ShapeDtypeStruct((8, pl.cdiv(peers, 128) * 128), jnp.int32)],
        in_specs=[far] * 5,
        out_specs=[pl.BlockSpec(memory_space=VMEM)] * 4,
        scratch_shapes=[
            pltpu.SMEM(table.shape, jnp.int32),
            VMEM((2, rows, width), jnp.bfloat16),
            VMEM((2, slots, rows, width), jnp.bfloat16),
            VMEM((4, rows, width), jnp.float32),
            pltpu.SemaphoreType.DMA((5,)),
        ],
        compiler_params=pltpu.CompilerParams(vmem_limit_bytes=8 << 20),
    )(
        table,
        stay(new_keys.reshape(rows, width)),
        stay(new_values.reshape(rows, width)),
        stay(pool_keys.reshape(slots, rows, width)),
        stay(pool_values.reshape(slots, rows, width)),
    )


def attend_kernel(peers, heads, uses, blocks, count, start, final, *rest):
    rest = list(rest)
    flags = rest.pop(0)[...] if blocks or any(use[3] == "c" for use in uses) else None
    if start:
        q_ref = rest.pop(0)
    else:
        qs, old_top, old_total, old_acc = rest[:4]
        rest = rest[4:]
    pieces = rest[:count]
    rest = rest[count:]
    if final:
        out_ref = rest.pop(0)
    elif start:
        qs, new_top, new_total, new_acc = rest[:4]
        rest = rest[4:]
    else:
        new_top, new_total, new_acc = rest[:3]
        rest = rest[3:]
    if start and final:
        qs = rest.pop(0)
    if start:
        wide = rest.pop(0)
    if final:
        ready, sems = rest[:2]
        rest = rest[2:]
    scores, rounded, chosen = rest
    me = lax.axis_index("seq")
    _, tokens, width = pieces[0].shape
    rows = qs.shape[1]
    group = rows // tokens
    factor = math.log2(math.e) / math.sqrt(width)
    if start:
        wide[...] = q_ref[...].astype(jnp.float32)
        for at in range(heads * group):
            picked = wide[pl.ds(at, tokens, stride=heads * group), :].astype(jnp.bfloat16)
            qs[at // group, at % group * tokens : (at % group + 1) * tokens, :] = picked
    slot = jnp.int32(0)
    sure = chosen.shape[0] - 1 - (peers - len(blocks))
    for at in range(max(sure, 0), chosen.shape[0] - 1):
        chosen[at] = jnp.zeros(chosen.shape[1:], chosen.dtype)
    for place, base, k, _ in blocks:
        chosen[slot] = pieces[place][base : base + 2 * heads]
        slot = jnp.minimum(slot + flags[0, k], chosen.shape[0] - 1)
    tiles = [(pieces[place], base, kind == "a" and k == 0) for place, base, k, kind in uses]
    allowed = []
    for _, _, k, kind in uses:
        if kind == "c":
            allowed.append(flags[0, k] == 1)
        else:
            allowed.append(None if k == 0 else (me ^ k) <= me)
    if blocks:
        tiles += [(chosen.at[at], 0, False) for at in range(chosen.shape[0] - 1)]
        allowed += [None if at < sure else slot > at for at in range(chosen.shape[0] - 1)]
    span = min(rows, 2 * tokens)
    folded = lambda x: x.reshape(tokens // 8, 8, span)
    turns = [(head, low) for head in range(heads) for low in range(0, rows, span)]
    peaks, totals, copies = {}, {}, []

    def score(turn):
        head, low = turns[turn]
        here = slice(low, low + span)
        queries = qs[head, here, :]
        peak = None
        for pair in range(0, len(tiles), 2):
            both = tiles[pair : pair + 2]
            keys = jnp.concatenate([ref[base + head] for ref, base, _ in both], axis=0)
            s = lax.dot_general(
                keys, queries, (((1,), (1,)), ((), ())), preferred_element_type=jnp.float32
            )
            for half, (_, _, causal) in enumerate(both):
                part = s[half * tokens : (half + 1) * tokens]
                if causal:
                    key_at = lax.broadcasted_iota(jnp.int32, part.shape, 0)
                    at = lax.broadcasted_iota(jnp.int32, part.shape, 1) % tokens
                    part = jnp.where(key_at <= at, part, neg_large)
                scores[turn % 2, pair + half] = part
                most = jnp.max(folded(part), axis=0)
                if allowed[pair + half] is not None:
                    most = jnp.where(allowed[pair + half], most, neg_large)
                peak = most if peak is None else jnp.maximum(peak, most)
        peak = jnp.max(peak, axis=0, keepdims=True) * factor
        if not start:
            peak = jnp.maximum(peak, old_top[head, :, here])
        peaks[turn] = peak

    def weigh(turn):
        peak = peaks[turn]
        sums = jnp.zeros((8, span), jnp.float32)
        for at in range(len(tiles)):
            level = peak
            if allowed[at] is not None:
                level = jnp.where(allowed[at], peak, -neg_large)
            p = jnp.exp2(scores[turn % 2, at] * factor - level)
            sums = sums + jnp.sum(folded(p), axis=0)
            rounded[turn % 2, at * tokens : (at + 1) * tokens, :] = p.astype(jnp.bfloat16)
        totals[turn] = jnp.sum(sums, axis=0, keepdims=True)

    def mix(turn):
        head, low = turns[turn]
        here = slice(low, low + span)
        peak, sums = peaks[turn], totals[turn]
        values = jnp.concatenate([ref[base + heads + head] for ref, base, _ in tiles], axis=1)
        mixed = jnp.dot(values, rounded[turn % 2], preferred_element_type=jnp.float32)
        if not start:
            fade = jnp.exp2(old_top[head, :, here] - peak)
            sums = sums + old_total[head, :, here] * fade
            mixed = mixed + old_acc[head, :, here] * fade
        if not final:
            new_top[head, :, here] = peak
            new_total[head, :, here] = sums
            new_acc[head, :, here] = mixed
            return
        whole = (mixed * (1.0 / sums)).astype(jnp.bfloat16)
        for inner in range(0, span, tokens):
            column = (head * group + (low + inner) // tokens) * width
            ready[:, column : column + width] = whole[:, inner : inner + tokens].T
        columns = pl.ds((head * group + low // tokens) * width, span // tokens * width)
        copies.append(
            pltpu.make_async_copy(ready.at[:, columns], out_ref.at[:, columns], sems.at[turn])
        )
        copies[-1].start()

    for turn in range(len(turns) + 2):
        if turn < len(turns):
            score(turn)
        if 0 <= turn - 1 < len(turns):
            weigh(turn - 1)
        if turn >= 2:
            mix(turn - 2)
    for copy in copies:
        copy.wait()


def attend(peers, flags, taken, queries, state, chunks, heads, start, final):
    tokens, query_heads, width = queries.shape
    rows = query_heads // heads * tokens
    span = min(rows, 2 * tokens)
    pieces, uses, blocks = [], [], []
    for array, base, k, kind in chunks:
        places = [at for at, held in enumerate(pieces) if held is array]
        if not places:
            places = [len(pieces)]
            pieces.append(array)
        (blocks if kind == "b" else uses).append((places[0], base, k, kind))
    asked = [flags] if blocks or any(use[3] == "c" for use in uses) else []
    inside = pl.BlockSpec(memory_space=VMEM)
    qs = ((heads, rows, width), jnp.bfloat16)
    carried = [
        ((heads, 1, rows), jnp.float32),
        ((heads, 1, rows), jnp.float32),
        ((heads, width, rows), jnp.float32),
    ]
    out = ((tokens, query_heads * width), jnp.bfloat16)
    tiles = len(uses) + (taken if blocks else 0)
    scratch = []
    if start and final:
        scratch.append(qs)
    if start:
        scratch.append(((tokens * query_heads, width), jnp.float32))
    if final:
        scratch.append(out)
    tail = [
        ((2, tiles, tokens, span), jnp.float32),
        ((2, tiles * tokens, span), jnp.bfloat16),
        ((taken + 1 if blocks else 1, 2 * heads, tokens, width), jnp.bfloat16),
    ]
    inputs = [queries.reshape(tokens * query_heads, width)] if start else list(state)
    outs = [out] if final else ([qs] if start else []) + carried
    bytes_of = lambda parts: sum(math.prod(s) * jnp.dtype(d).itemsize for s, d in parts)
    moved = bytes_of([(x.shape, x.dtype) for x in inputs + pieces] + outs)
    work = 2 * tiles * heads * rows * 2 * tokens * width
    result = pl.pallas_call(
        functools.partial(attend_kernel, peers, heads, uses, blocks, len(pieces), start, final),
        out_shape=[jax.ShapeDtypeStruct(s, d) for s, d in outs],
        in_specs=[inside] * (len(asked) + len(inputs) + len(pieces)),
        out_specs=[pl.BlockSpec(memory_space=pltpu.HBM)] if final else [inside] * len(outs),
        scratch_shapes=[VMEM(s, d) for s, d in scratch]
        + ([pltpu.SemaphoreType.DMA((heads * rows // span,))] if final else [])
        + [VMEM(s, d) for s, d in tail],
        cost_estimate=pl.CostEstimate(
            flops=work, bytes_accessed=moved, transcendentals=work // (4 * width)
        ),
        compiler_params=pltpu.CompilerParams(
            vmem_limit_bytes=(8 << 20) + moved + bytes_of(scratch + tail)
        ),
    )(*asked, *inputs, *pieces)
    if final:
        return result[0]
    return result if start else [state[0]] + list(result)


def move(x, n, k, sends=lambda i: True):
    return lax.ppermute(x, "seq", [(i, i ^ k) for i in range(n) if sends(i)])


def plan(n):
    far = range(4, n, 4)
    lows = (3, 1, 2)
    new, block = "a", "b"
    waves = lambda part: [("move", part, k + low, k) for k in far for low in lows]
    some = lambda numbers: [
        ("work", [(part, k) for part, k in numbers[at : at + 6]])
        for at in range(0, len(numbers), 6)
    ]
    one = lambda part, low, source: [
        ("move", part, k + low, k + source if source is not None else 0) for k in far
    ]
    events = []
    events += one(block, 0, None)
    events += [("move", "d", 1, 0)]
    events += [("move", "d", 2, 0)]
    events += [("work", [(new, 0)])]
    events += one(new, 0, None)
    events += waves(block)
    events += [("move", new, k + 1, k) for k in far]
    events += [("move", "d", 3, 2)]
    events += [("move", new, k + low, k) for k in far for low in (3, 2)]
    events += some([(new, 1), (new, 2)] + [(new, k) for k in far])
    events += [("work", [(block, k) for k in range(n) if k != 3])]
    ends = [(new, 3), ("c", 3)] + [(new, k + low) for k in far for low in lows]
    events += some(ends)
    later = []
    return events, later


def body(n, queries, new_keys, new_values, pool_keys, pool_values, table):
    heads = new_keys.shape[1]
    table = stay(table)
    events, _ = plan(n)
    last = max(at for at, event in enumerate(events) if event[0] == "work")
    own, fresh, block, flags = pack(n, table, new_keys, new_values, pool_keys, pool_values)
    moved = {("d", 0): own, ("a", 0): fresh, ("b", 0): block}
    held = {("a", 0): (fresh, 0), ("b", 0): (block, 0)}
    state = None
    for number, event in enumerate(events):
        if event[0] == "move":
            _, part, k, source = event
            hop = k ^ source
            sends = lambda i: True
            if part == "a":
                sends = lambda i: i ^ hop > (i ^ hop) ^ k
            if (part, source) in moved:
                piece = moved[(part, source)]
            else:
                piece = moved[("d", source)][2 * heads * (part == "b") :][: 2 * heads]
            got = move(piece, n, hop, sends)
            moved[(part, k)] = got
            if part == "d":
                held[("a", k)] = (got, 0)
                held[("b", k)] = (got, 2 * heads)
            else:
                held[(part, k)] = (got, 0)
        else:
            chunks = [held[("a" if kind == "a" else "b", k)] + (k, kind) for kind, k in event[1]]
            state = attend(
                n,
                flags,
                table.shape[0],
                queries,
                state,
                chunks,
                heads,
                state is None,
                number == last,
            )
    return state


def solution(mesh):
    in_specs = (
        P(("grp", "seq"), "head", None),
        P(("grp", "seq"), "head", None),
        P(("grp", "seq"), "head", None),
        P(("grp", "seq"), None, "head", None),
        P(("grp", "seq"), None, "head", None),
        P("grp"),
    )
    out_specs = P(("grp", "seq"), "head")
    n = mesh.shape["seq"]
    return jax.shard_map(
        functools.partial(body, n),
        mesh=mesh,
        in_specs=in_specs,
        out_specs=out_specs,
        check_vma=False,
    )
```
